32 devices in a mesh: gx: 4 (over z), gy: 4 (over y, x), gz: 2 (over core).
Axes of the slice: x: 2, y: 2, z: 4, core: 2. Of those that a mesh axis runs over, the one named last changes fastest.
Arguments:
- species_field: float32 [8, 384, 6144], P('gz', 'gx', 'gy'), may hold values from -24 to 24
- start_first: float32 [384, 96], replicated, may hold values from -0.3125 to 0.3125
- start_second: float32 [384, 96], replicated, may hold values from -0.3125 to 0.3125
Outputs:
- factor_first: float32 [384, 96], replicated
- factor_second: float32 [384, 96], replicated
- core_tensor: float32 [16, 8, 96, 96], P('gx', 'gz', 'gy')
The draws below stay inside these ranges and needn't reach their ends.
All inputs are finite; a program needn't handle non-finite values.
Results may differ from the reference program's by a relative error of at most 0.0003.
Values sent between devices are 32-bit elements; how exact they have to be, the bound alone decides.
A program may use at most 64 MiB of HBM per device.

```python
import math
import jax
import jax.numpy as jnp
from jax import lax

S = 16
NX = 384
NY = 384
RANK = 96
ITERS = 2
NZ = 8


def scaled_range(subkey, length_of, lowest, highest):
    return jnp.exp(jax.random.uniform(subkey, (length_of,), jnp.float32, math.log(lowest), math.log(highest)))


def draw_species_field(key, part):
    subkeys = jax.random.split(key, 9)
    signal_rank = max(RANK // 2, 1)
    left_factor = jax.random.truncated_normal(subkeys[0], -4.0, 4.0, (NX, signal_rank), jnp.float32)
    left_factor = left_factor * scaled_range(subkeys[1], signal_rank, 0.5, 2.0)[None, :] / math.sqrt(signal_rank)
    right_factor = jax.random.truncated_normal(subkeys[2], -4.0, 4.0, (NY, signal_rank), jnp.float32)
    right_factor = right_factor * scaled_range(subkeys[3], signal_rank, 0.5, 2.0)[None, :] / math.sqrt(signal_rank)
    inner_core = jax.random.truncated_normal(subkeys[4], -4.0, 4.0, (NZ, signal_rank, signal_rank, S), jnp.float32)
    region = jax.random.uniform(subkeys[5], (NZ, S), jnp.float32, 0.4, 1.6)
    inner_core = inner_core * region[:, None, None, :]
    mixed = jnp.einsum('zabs,ia->zibs', inner_core, left_factor)
    signal = jnp.einsum('zibs,jb->zijs', mixed, right_factor)
    row_scale = scaled_range(subkeys[6], NX, 0.5, 1.5)
    column_scale = scaled_range(subkeys[7], NY, 0.5, 1.5)
    noise_part = jax.random.truncated_normal(subkeys[8], -4.0, 4.0, (NZ, NX, NY, S), jnp.float32)
    noise_part = noise_part * (row_scale[:, None] * column_scale[None, :])[None, :, :, None]
    whole = jnp.clip(signal + noise_part, -24.0, 24.0)
    return whole.reshape(NZ, NX, NY * S).astype(jnp.float32)


def centred(stream_key, extent, deviation, bound, dtype=jnp.bfloat16):
    return jnp.clip(deviation * jax.random.normal(stream_key, extent, jnp.float32), -bound, bound).astype(dtype)


def setup_inputs(seed: int = 0) -> dict:
    key_list = jax.random.split(jax.random.key(seed), 4)
    return {
        "species_field": draw_species_field(jax.random.fold_in(key_list[3], 71), 0),
        "start_first": centred(key_list[1], (NX, RANK), NX ** -0.5, 0.3125, jnp.float32),
        "start_second": centred(key_list[2], (NY, RANK), NY ** -0.5, 0.3125, jnp.float32),
    }


exact_precision = lax.Precision.HIGHEST

def power_steps(gram, start):
    current = start
    for turn in range(ITERS):
        images = jnp.dot(gram, current, precision=exact_precision)
        cross_gram = jnp.dot(images.T, images, precision=exact_precision)
        lower_factor = jnp.linalg.cholesky(cross_gram)
        current = lax.linalg.triangular_solve(lower_factor, images, left_side=False, lower=True, transpose_a=True)
    return current

def reference(species_field, start_first, start_second):
    field = species_field.reshape(NZ, NX, NY, S)
    gram_first = jnp.einsum('zics,zjcs->ij', field, field, precision=exact_precision)
    factor_first = power_steps(gram_first, start_first)
    projected = jnp.einsum('zics,ir->zrcs', field, factor_first, precision=exact_precision)
    gram_second = jnp.einsum('zrjs,zrks->jk', projected, projected, precision=exact_precision)
    factor_second = power_steps(gram_second, start_second)
    core_tensor = jnp.einsum('zrjs,jq->szrq', projected, factor_second, precision=exact_precision)
    return (factor_first, factor_second, core_tensor)
```

```python
import functools

import jax
import jax.numpy as jnp
from jax import lax
from jax.experimental import pallas as pl
from jax.experimental.pallas import tpu as pltpu
from jax.sharding import PartitionSpec as P

S = 16
ITERS = 2
PANEL = 16
MESH = pl.DeviceIdType.MESH
VMEM = pl.BlockSpec(memory_space=pltpu.VMEM)

exact_precision = lax.Precision.HIGHEST


def dot_dims(a, b, contract_a, contract_b):
    return lax.dot_general(
        a, b, (((contract_a,), (contract_b,)), ((), ())),
        precision=exact_precision, preferred_element_type=jnp.float32,
    )


def partners(n, me):
    if n == 4:
        return [3 - me, lax.rem(me + 2, 4), me + 1 - 2 * lax.rem(me, 2)]
    return [lax.rem(me + d, n) for d in range(1, n)]


def send(src, dst, send_sem, recv_sem, target):
    copy = pltpu.make_async_remote_copy(
        src_ref=src, dst_ref=dst, send_sem=send_sem, recv_sem=recv_sem,
        device_id=target, device_id_type=MESH,
    )
    copy.start()
    return copy


def greet(targets):
    barrier = pltpu.get_barrier_semaphore()
    for target in targets:
        pl.semaphore_signal(barrier, inc=1, device_id=target, device_id_type=MESH)
    pl.semaphore_wait(barrier, len(targets))


def all_reduce_kernel(axes, sizes, splits, x_ref, o_ref, *scratch):
    levels = len(axes)
    landing, totals = scratch[:levels], scratch[levels : 2 * levels - 1]
    send_sems, recv_sems = scratch[2 * levels - 1 :]
    me = [lax.axis_index(axis) for axis in axes]
    peers = [partners(n, m) for n, m in zip(sizes, me)]
    greet([{axis: p} for axis, ps in zip(axes, peers) for p in ps])

    spot = [m if split > 1 else 0 for m, split in zip(me, splits)]
    sem = 0
    held = x_ref
    for level in range(levels):
        axis, n, split = axes[level], sizes[level], splits[level]
        land = landing[level]
        copies = []
        for p in peers[level]:
            src = held.at[p] if split > 1 else held.at[0]
            copies.append(send(src, land.at[me[level]], send_sems.at[sem], recv_sems.at[sem], {axis: p}))
            sem += 1
        land[me[level]] = held[spot[level]]
        for copy in copies:
            copy.wait()
        total = land[0]
        for source in range(1, n):
            total = total + land[source]
        if level < levels - 1:
            totals[level][...] = total
            held = totals[level]
        else:
            o_ref[tuple(spot)] = total

    for level in reversed(range(levels)):
        if splits[level] == 1:
            continue
        block = o_ref.at[tuple(spot[: level + 1])]
        copies = []
        for p in peers[level]:
            copies.append(send(block, block, send_sems.at[sem], recv_sems.at[sem], {axes[level]: p}))
            sem += 1
        for copy in copies:
            copy.wait()


def all_reduce(x, axes, sizes, collective_id):
    rows, columns = x.shape
    splits = []
    for n in sizes:
        splits.append(n if rows % n == 0 else 1)
        rows //= splits[-1]
    blocked = x.reshape(*splits, rows, columns)
    landing = [
        pltpu.VMEM((n, *splits[level + 1 :], rows, columns), jnp.float32)
        for level, n in enumerate(sizes)
    ]
    totals = [pltpu.VMEM((*splits[level + 1 :], rows, columns), jnp.float32) for level in range(len(sizes) - 1)]
    count = sum(n - 1 for n in sizes) + sum(n - 1 for n, split in zip(sizes, splits) if split > 1)
    out = pl.pallas_call(
        functools.partial(all_reduce_kernel, axes, sizes, splits),
        out_shape=jax.ShapeDtypeStruct(blocked.shape, jnp.float32),
        in_specs=[VMEM],
        out_specs=VMEM,
        scratch_shapes=landing + totals + [pltpu.SemaphoreType.DMA((count,)), pltpu.SemaphoreType.DMA((count,))],
        compiler_params=pltpu.CompilerParams(collective_id=collective_id, has_side_effects=True),
    )(blocked)
    return out.reshape(x.shape)


def fibres_kernel(n, x_ref, o_ref, send_sems, recv_sems):
    me = lax.axis_index("gx")
    depth, rows, width = x_ref.shape[0], x_ref.shape[1], o_ref.shape[-1]
    peers = partners(n, me)
    greet([{"gx": p} for p in peers])
    copies = []
    for turn, p in enumerate(peers):
        columns = pl.ds(pl.multiple_of(p * width, width), width)
        copies.append(
            send(x_ref.at[:, :, columns], o_ref.at[:, me], send_sems.at[turn], recv_sems.at[turn], {"gx": p})
        )
    own = pl.ds(pl.multiple_of(me * width, width), width)
    for level in range(depth):
        o_ref[level, me] = x_ref[level, :, own]
    for copy in copies:
        copy.wait()


def gather_fibres(field, n):
    depth, rows, columns = field.shape
    width = columns // n
    if width % 128:
        return lax.all_to_all(field, "gx", split_axis=2, concat_axis=1, tiled=True)
    out = pl.pallas_call(
        functools.partial(fibres_kernel, n),
        out_shape=jax.ShapeDtypeStruct((depth, n, rows, width), jnp.float32),
        in_specs=[VMEM],
        out_specs=VMEM,
        scratch_shapes=[pltpu.SemaphoreType.DMA((n - 1,)), pltpu.SemaphoreType.DMA((n - 1,))],
        compiler_params=pltpu.CompilerParams(collective_id=0, has_side_effects=True),
    )(field)
    return out.reshape(depth, n * rows, width)


def exchange_kernel(nx, ny, x_ref, o_ref, send_sems, recv_sems):
    mx, my = lax.axis_index("gx"), lax.axis_index("gy")
    peers = [(px, my) for px in partners(nx, mx)]
    for py in partners(ny, my):
        peers += [(px, py) for px in partners(nx, mx) + [mx]]
    greet([{"gx": px, "gy": py} for px, py in peers])
    copies = []
    for turn, (px, py) in enumerate(peers):
        copies.append(
            send(x_ref.at[py, px], o_ref.at[my, mx], send_sems.at[turn], recv_sems.at[turn], {"gx": px, "gy": py})
        )
    o_ref[my, mx] = x_ref[my, mx]
    for copy in copies:
        copy.wait()


def exchange(blocks):
    ny, nx = blocks.shape[:2]
    count = nx * ny - 1
    return pl.pallas_call(
        functools.partial(exchange_kernel, nx, ny),
        out_shape=jax.ShapeDtypeStruct(blocks.shape, jnp.float32),
        in_specs=[VMEM],
        out_specs=VMEM,
        scratch_shapes=[pltpu.SemaphoreType.DMA((count,)), pltpu.SemaphoreType.DMA((count,))],
        compiler_params=pltpu.CompilerParams(collective_id=1, has_side_effects=True),
    )(blocks)


def inverse_lower(cross):
    rank = cross.shape[0]
    panel = PANEL if rank % PANEL == 0 else 8
    row = lax.broadcasted_iota(jnp.int32, (rank, rank), 0)
    column = lax.broadcasted_iota(jnp.int32, (rank, rank), 1)
    rest = cross
    rest_inverse = jnp.where(row == column, 1.0, 0.0).astype(jnp.float32)
    local_row = lax.broadcasted_iota(jnp.int32, (panel, rank), 0)
    done = []
    for start in range(0, rank, panel):
        upper = rest[:panel]
        inverse = rest_inverse[:panel]
        columns = [
            jnp.broadcast_to(upper[:, start + j : start + j + 1], (panel, rank)) for j in range(panel)
        ]
        diagonal = jnp.ones((panel, rank), jnp.float32)
        for j in range(panel):
            pivot = jnp.broadcast_to(columns[j][j : j + 1], (panel, rank))
            diagonal = jnp.where(local_row == j, pivot, diagonal)
            if j == panel - 1:
                break
            factor = jnp.where(local_row > j, columns[j] * (1.0 / pivot), 0.0)
            for other in range(j + 1, panel):
                columns[other] = columns[other] - factor * columns[other][j : j + 1]
            upper = upper - factor * upper[j : j + 1]
            inverse = inverse - factor * inverse[j : j + 1]
        done.append(inverse * (1.0 / jnp.sqrt(diagonal)))
        if start + panel < rank:
            scaled = upper / diagonal
            update = dot_dims(scaled, jnp.concatenate([upper, inverse], axis=1), 0, 0)
            after = start + panel
            rest = rest[panel:] - update[after:, :rank]
            rest_inverse = rest_inverse[panel:] - update[after:, rank:]
    return jnp.concatenate(done, axis=0)


def power_kernel(gram_ref, start_ref, out_ref):
    current = start_ref[...]
    for turn in range(ITERS):
        images = dot_dims(gram_ref[...], current, 1, 0)
        cross = dot_dims(images, images, 0, 0)
        current = dot_dims(images, inverse_lower(cross), 1, 1)
    out_ref[...] = current


def leading(gram, start):
    return pl.pallas_call(
        power_kernel,
        out_shape=jax.ShapeDtypeStruct(start.shape, jnp.float32),
        in_specs=[VMEM, VMEM],
        out_specs=VMEM,
    )(gram, start)


def local(nx, ny, nz, species_field, start_first, start_second):
    axes, sizes = ("gz", "gy", "gx"), (nz, ny, nx)
    fibres = gather_fibres(species_field, nx)
    partial_gram = jnp.einsum("zic,zjc->ij", fibres, fibres, precision=exact_precision)
    gram_first = all_reduce(partial_gram, axes, sizes, 2)
    factor_first = leading(gram_first, start_first)

    depth = fibres.shape[0]
    cells = fibres.shape[2] // S
    rank = start_first.shape[1]
    species, ranks = S // nx, rank // ny
    projected = jnp.einsum("zim,ir->zmr", fibres, factor_first, precision=exact_precision)
    blocks = projected.reshape(depth, cells, nx, species, ny, ranks)
    blocks = blocks.transpose(4, 2, 1, 3, 0, 5).reshape(ny, nx, cells, species * depth * ranks)
    columns = exchange(blocks)
    columns = columns.reshape(ny * nx * cells, species * depth * ranks)
    partial_second = dot_dims(columns, columns, 1, 1)
    gram_second = all_reduce(partial_second, axes, sizes, 3)
    factor_second = leading(gram_second, start_second)
    core = dot_dims(columns, factor_second, 0, 0)
    core = core.reshape(species, depth, ranks, factor_second.shape[1])
    return (factor_first, factor_second, core)


def solution(mesh):
    return jax.shard_map(
        functools.partial(local, mesh.shape["gx"], mesh.shape["gy"], mesh.shape["gz"]),
        mesh=mesh,
        in_specs=(P("gz", "gx", "gy"), P(), P()),
        out_specs=(P(), P(), P("gx", "gz", "gy", None)),
        check_vma=False,
    )
```

```python
import functools

import jax
import jax.numpy as jnp
from jax import lax
from jax.experimental import pallas as pl
from jax.experimental.pallas import tpu as pltpu
from jax.sharding import PartitionSpec as P

S = 16
ITERS = 2
PANEL = 16
LANES = 128
MESH = pl.DeviceIdType.MESH
VMEM = pl.BlockSpec(memory_space=pltpu.VMEM)

exact_precision = lax.Precision.HIGHEST


def dot_dims(a, b, contract_a, contract_b):
    return lax.dot_general(
        a, b, (((contract_a,), (contract_b,)), ((), ())),
        precision=exact_precision, preferred_element_type=jnp.float32,
    )


def partners(n, me):
    if n == 4:
        return [3 - me, lax.rem(me + 2, 4), me + 1 - 2 * lax.rem(me, 2)]
    return [lax.rem(me + d, n) for d in range(1, n)]


def send(src, dst, send_sem, recv_sem, target):
    copy = pltpu.make_async_remote_copy(
        src_ref=src, dst_ref=dst, send_sem=send_sem, recv_sem=recv_sem,
        device_id=target, device_id_type=MESH,
    )
    copy.start()
    return copy


def greet(targets):
    barrier = pltpu.get_barrier_semaphore()
    for target in targets:
        pl.semaphore_signal(barrier, inc=1, device_id=target, device_id_type=MESH)
    pl.semaphore_wait(barrier, len(targets))


def all_reduce_kernel(axes, sizes, splits, x_ref, o_ref, *scratch):
    levels = len(axes)
    landing, totals = scratch[:levels], scratch[levels : 2 * levels - 1]
    send_sems, recv_sems = scratch[2 * levels - 1 :]
    me = [lax.axis_index(axis) for axis in axes]
    peers = [partners(n, m) for n, m in zip(sizes, me)]
    greet([{axis: p} for axis, ps in zip(axes, peers) for p in ps])

    spot = [m if split > 1 else 0 for m, split in zip(me, splits)]
    sem = 0
    held = x_ref
    for level in range(levels):
        axis, n, split = axes[level], sizes[level], splits[level]
        land = landing[level]
        copies = []
        for p in peers[level]:
            src = held.at[p] if split > 1 else held.at[0]
            copies.append(send(src, land.at[me[level]], send_sems.at[sem], recv_sems.at[sem], {axis: p}))
            sem += 1
        land[me[level]] = held[spot[level]]
        for copy in copies:
            copy.wait()
        total = land[0]
        for source in range(1, n):
            total = total + land[source]
        if level < levels - 1:
            totals[level][...] = total
            held = totals[level]
        else:
            o_ref[tuple(spot)] = total

    for level in reversed(range(levels)):
        if splits[level] == 1:
            continue
        block = o_ref.at[tuple(spot[: level + 1])]
        copies = []
        for p in peers[level]:
            copies.append(send(block, block, send_sems.at[sem], recv_sems.at[sem], {axes[level]: p}))
            sem += 1
        for copy in copies:
            copy.wait()


def all_reduce(x, axes, sizes, collective_id):
    rows, columns = x.shape
    splits = []
    for n in sizes:
        splits.append(n if rows % n == 0 else 1)
        rows //= splits[-1]
    blocked = x.reshape(*splits, rows, columns)
    landing = [
        pltpu.VMEM((n, *splits[level + 1 :], rows, columns), jnp.float32)
        for level, n in enumerate(sizes)
    ]
    totals = [pltpu.VMEM((*splits[level + 1 :], rows, columns), jnp.float32) for level in range(len(sizes) - 1)]
    count = sum(n - 1 for n in sizes) + sum(n - 1 for n, split in zip(sizes, splits) if split > 1)
    out = pl.pallas_call(
        functools.partial(all_reduce_kernel, axes, sizes, splits),
        out_shape=jax.ShapeDtypeStruct(blocked.shape, jnp.float32),
        in_specs=[VMEM],
        out_specs=VMEM,
        scratch_shapes=landing + totals + [pltpu.SemaphoreType.DMA((count,)), pltpu.SemaphoreType.DMA((count,))],
        compiler_params=pltpu.CompilerParams(collective_id=collective_id, has_side_effects=True),
    )(blocked)
    return out.reshape(x.shape)


def fibres_kernel(n, x_ref, o_ref, send_sems, recv_sems):
    me = lax.axis_index("gx")
    depth, rows, width = x_ref.shape[0], x_ref.shape[1], o_ref.shape[-1]
    peers = partners(n, me)
    greet([{"gx": p} for p in peers])
    copies = []
    for turn, p in enumerate(peers):
        columns = pl.ds(pl.multiple_of(p * width, width), width)
        copies.append(
            send(x_ref.at[:, :, columns], o_ref.at[:, me], send_sems.at[turn], recv_sems.at[turn], {"gx": p})
        )
    own = pl.ds(pl.multiple_of(me * width, width), width)
    for level in range(depth):
        o_ref[level, me] = x_ref[level, :, own]
    for copy in copies:
        copy.wait()


def gather_fibres(field, n):
    depth, rows, columns = field.shape
    width = columns // n
    if width % 128:
        return lax.all_to_all(field, "gx", split_axis=2, concat_axis=1, tiled=True)
    out = pl.pallas_call(
        functools.partial(fibres_kernel, n),
        out_shape=jax.ShapeDtypeStruct((depth, n, rows, width), jnp.float32),
        in_specs=[VMEM],
        out_specs=VMEM,
        scratch_shapes=[pltpu.SemaphoreType.DMA((n - 1,)), pltpu.SemaphoreType.DMA((n - 1,))],
        compiler_params=pltpu.CompilerParams(collective_id=0, has_side_effects=True),
    )(field)
    return out.reshape(depth, n * rows, width)


def exchange_kernel(nx, ny, x_ref, o_ref, send_sems, recv_sems):
    mx, my = lax.axis_index("gx"), lax.axis_index("gy")
    peers = [(px, my) for px in partners(nx, mx)]
    for py in partners(ny, my):
        peers += [(px, py) for px in partners(nx, mx) + [mx]]
    greet([{"gx": px, "gy": py} for px, py in peers])
    copies = []
    for turn, (px, py) in enumerate(peers):
        copies.append(
            send(x_ref.at[py, px], o_ref.at[my, mx], send_sems.at[turn], recv_sems.at[turn], {"gx": px, "gy": py})
        )
    o_ref[my, mx] = x_ref[my, mx]
    for copy in copies:
        copy.wait()


def exchange(blocks):
    ny, nx = blocks.shape[:2]
    count = nx * ny - 1
    return pl.pallas_call(
        functools.partial(exchange_kernel, nx, ny),
        out_shape=jax.ShapeDtypeStruct(blocks.shape, jnp.float32),
        in_specs=[VMEM],
        out_specs=VMEM,
        scratch_shapes=[pltpu.SemaphoreType.DMA((count,)), pltpu.SemaphoreType.DMA((count,))],
        compiler_params=pltpu.CompilerParams(collective_id=1, has_side_effects=True),
    )(blocks)


def inverse_lower(cross):
    rank = cross.shape[0]
    panel = PANEL if rank % PANEL == 0 else 8
    row = lax.broadcasted_iota(jnp.int32, (rank, rank), 0)
    column = lax.broadcasted_iota(jnp.int32, (rank, rank), 1)
    rest = cross
    rest_inverse = jnp.where(row == column, 1.0, 0.0).astype(jnp.float32)
    local_row = lax.broadcasted_iota(jnp.int32, (panel, rank), 0)
    done = []
    for start in range(0, rank, panel):
        upper = rest[:panel]
        inverse = rest_inverse[:panel]
        columns = [
            jnp.broadcast_to(upper[:, start + j : start + j + 1], (panel, rank)) for j in range(panel)
        ]
        diagonal = jnp.ones((panel, rank), jnp.float32)
        for j in range(panel):
            pivot = jnp.broadcast_to(columns[j][j : j + 1], (panel, rank))
            diagonal = jnp.where(local_row == j, pivot, diagonal)
            if j == panel - 1:
                break
            factor = jnp.where(local_row > j, columns[j] * (1.0 / pivot), 0.0)
            for other in range(j + 1, panel):
                columns[other] = columns[other] - factor * columns[other][j : j + 1]
            upper = upper - factor * upper[j : j + 1]
            inverse = inverse - factor * inverse[j : j + 1]
        done.append(inverse * (1.0 / jnp.sqrt(diagonal)))
        if start + panel < rank:
            scaled = upper / diagonal
            update = dot_dims(scaled, jnp.concatenate([upper, inverse], axis=1), 0, 0)
            after = start + panel
            rest = rest[panel:] - update[after:, :rank]
            rest_inverse = rest_inverse[panel:] - update[after:, rank:]
    return jnp.concatenate(done, axis=0)


def power_general_kernel(gram_ref, start_ref, out_ref):
    current = start_ref[...]
    for turn in range(ITERS):
        images = dot_dims(gram_ref[...], current, 1, 0)
        cross = dot_dims(images, images, 0, 0)
        current = dot_dims(images, inverse_lower(cross), 1, 1)
    out_ref[...] = current


def leading(gram, start):
    return pl.pallas_call(
        power_general_kernel,
        out_shape=jax.ShapeDtypeStruct(start.shape, jnp.float32),
        in_specs=[VMEM, VMEM],
        out_specs=VMEM,
    )(gram, start)


def local_general(nx, ny, nz, species_field, start_first, start_second):
    axes, sizes = ("gz", "gy", "gx"), (nz, ny, nx)
    fibres = gather_fibres(species_field, nx)
    partial_gram = jnp.einsum("zic,zjc->ij", fibres, fibres, precision=exact_precision)
    gram_first = all_reduce(partial_gram, axes, sizes, 2)
    factor_first = leading(gram_first, start_first)

    depth = fibres.shape[0]
    cells = fibres.shape[2] // S
    rank = start_first.shape[1]
    species, ranks = S // nx, rank // ny
    projected = jnp.einsum("zim,ir->zmr", fibres, factor_first, precision=exact_precision)
    blocks = projected.reshape(depth, cells, nx, species, ny, ranks)
    blocks = blocks.transpose(4, 2, 1, 3, 0, 5).reshape(ny, nx, cells, species * depth * ranks)
    columns = exchange(blocks)
    columns = columns.reshape(ny * nx * cells, species * depth * ranks)
    partial_second = dot_dims(columns, columns, 1, 1)
    gram_second = all_reduce(partial_second, axes, sizes, 3)
    factor_second = leading(gram_second, start_second)
    core = dot_dims(columns, factor_second, 0, 0)
    core = core.reshape(species, depth, ranks, factor_second.shape[1])
    return (factor_first, factor_second, core)


def upper_blocks(count):
    return [(a, b) for a in range(count) for b in range(a, count)]


def add_gram(gram_ref, parts, contract, first):
    for slot, (a, b) in enumerate(upper_blocks(len(parts))):
        block = pl.ds(slot * LANES, LANES)
        term = dot_dims(parts[a], parts[b], contract, contract)
        gram_ref[block, :] = term if first else gram_ref[block, :] + term


def times_gram(current, gram_ref):
    count = current.shape[1] // LANES
    sums = [None] * count
    for slot, (a, b) in enumerate(upper_blocks(count)):
        block = gram_ref[slot * LANES : (slot + 1) * LANES, :]
        terms = [(b, a, 0)] if a == b else [(b, a, 0), (a, b, 1)]
        for to, of, contract in terms:
            term = dot_dims(current[:, of * LANES : (of + 1) * LANES], block, 1, contract)
            sums[to] = term if sums[to] is None else sums[to] + term
    return jnp.concatenate(sums, axis=1)


def power_steps(gram_ref, current):
    for turn in range(ITERS):
        images = times_gram(current, gram_ref)
        cross = dot_dims(images, images, 1, 1)
        current = dot_dims(inverse_lower(cross), images, 1, 0)
    return current


def first_power_kernel(gram_ref, start_ref, out_ref):
    out_ref[...] = power_steps(gram_ref, start_ref[...])


def second_power_kernel(groups, cells, gram_ref, start_ref, rows_ref, out_ref, core_ref):
    extent = start_ref.shape[1]
    chunks = extent // LANES
    true = lax.broadcasted_iota(jnp.int32, (extent, extent), 0)
    held = lax.broadcasted_iota(jnp.int32, (extent, extent), 1)
    shift = cells.bit_length() - 1
    chunk = lax.shift_right_logical(held, LANES.bit_length() - 1)
    group = lax.shift_right_logical(held & (LANES - 1), shift)
    order = jnp.where(true == (group * chunks + chunk) * cells + (held & (cells - 1)), 1.0, 0.0)
    current = power_steps(gram_ref, dot_dims(start_ref[...], order, 1, 0))
    out_ref[...] = dot_dims(current, order, 1, 1)
    core_ref[...] = dot_dims(rows_ref[...], current, 1, 1)


def species_major(block, order):
    high = block.astype(jnp.bfloat16)
    left = block - high.astype(jnp.float32)
    middle = left.astype(jnp.bfloat16)
    low = (left - middle.astype(jnp.float32)).astype(jnp.bfloat16)
    moved = [
        lax.dot_general(part, order, (((1,), (0,)), ((), ())), preferred_element_type=jnp.float32)
        for part in (high, middle, low)
    ]
    return (moved[0] + moved[1]) + moved[2]


def first_kernel(n, x_ref, fibres_ref, gram_ref, packed, send_sems, recv_sems):
    me = lax.axis_index("gx")
    depth, rows, columns = x_ref.shape
    span = n * LANES
    cells = span // S
    width = columns // n
    peers = partners(n, me)
    greet([{"gx": p} for p in peers])
    source = lax.broadcasted_iota(jnp.int32, (span, span), 0)
    target = lax.broadcasted_iota(jnp.int32, (span, span), 1)
    species = lax.shift_right_logical(target, cells.bit_length() - 1)
    order = jnp.where(source == (target & (cells - 1)) * S + species, 1.0, 0.0).astype(jnp.bfloat16)
    copies = []
    for level in range(depth):
        for chunk in range(columns // span):
            moved = species_major(x_ref[level, :, chunk * span : (chunk + 1) * span], order)
            lanes = pl.ds(chunk * LANES, LANES)
            for p in range(n):
                packed[level, p, :, lanes] = moved[:, p * LANES : (p + 1) * LANES]
        for turn, p in enumerate(peers):
            sem = level * (n - 1) + turn
            copies.append(
                send(packed.at[level, p], fibres_ref.at[level, me], send_sems.at[sem], recv_sems.at[sem], {"gx": p})
            )
        fibres_ref[level, me] = packed[level, me]
    for level in range(depth):
        for copy in copies[level * (n - 1) : (level + 1) * (n - 1)]:
            copy.wait()
        whole = fibres_ref[level].reshape(n * rows, width)
        parts = [whole[a : a + LANES] for a in range(0, n * rows, LANES)]
        add_gram(gram_ref, parts, 1, level == 0)


def first_stage(field, n):
    depth, rows, columns = field.shape
    width = columns // n
    blocks = len(upper_blocks(n * rows // LANES))
    count = depth * (n - 1)
    return pl.pallas_call(
        functools.partial(first_kernel, n),
        out_shape=(
            jax.ShapeDtypeStruct((depth, n, rows, width), jnp.float32),
            jax.ShapeDtypeStruct((blocks * LANES, LANES), jnp.float32),
        ),
        in_specs=[VMEM],
        out_specs=(VMEM, VMEM),
        scratch_shapes=[
            pltpu.VMEM((depth, n, rows, width), jnp.float32),
            pltpu.SemaphoreType.DMA((count,)),
            pltpu.SemaphoreType.DMA((count,)),
        ],
        compiler_params=pltpu.CompilerParams(collective_id=0, has_side_effects=True),
    )(field)


def second_kernel(n, cells, factor_ref, fibres_ref, rows_ref, gram_ref, packed, land, send_sems, recv_sems):
    me = lax.axis_index("gy")
    depth, ranks, width = packed.shape[0], packed.shape[2], packed.shape[3]
    peers = partners(n, me)
    greet([{"gy": p} for p in peers])
    copies = []
    for level in range(depth):
        whole = fibres_ref[level].reshape(factor_ref.shape[1], width)
        projected = dot_dims(factor_ref[...], whole, 1, 0)
        packed[level] = projected.reshape(n, ranks, width)
        for turn, p in enumerate(peers):
            sem = level * (n - 1) + turn
            copies.append(
                send(packed.at[level, p], land.at[me, level], send_sems.at[sem], recv_sems.at[sem], {"gy": p})
            )
        land[me, level] = packed[level, me]
    lane_group = lax.shift_right_logical(
        lax.broadcasted_iota(jnp.int32, (ranks, LANES), 1), cells.bit_length() - 1
    )
    for level in range(depth):
        for copy in copies[level * (n - 1) : (level + 1) * (n - 1)]:
            copy.wait()
        for chunk in range(width // LANES):
            lanes = pl.ds(chunk * LANES, LANES)
            pieces = [land[t, level, :, lanes] for t in range(n)]
            for s in range(n):
                merged = pieces[s]
                for t in range(n):
                    if t != s:
                        turned = pltpu.roll(pieces[t], cells * ((t - s) % n), 1)
                        merged = jnp.where(lane_group == t, turned, merged)
                rows_ref[s, level, :, lanes] = merged
        whole = rows_ref[:, level].reshape(n * ranks, width)
        parts = [whole[:, a : a + LANES] for a in range(0, width, LANES)]
        add_gram(gram_ref, parts, 0, level == 0)


def second_stage(factor, fibres, n, cells):
    depth, _, _, width = fibres.shape
    ranks = factor.shape[0] // n
    blocks = len(upper_blocks(width // LANES))
    count = depth * (n - 1)
    return pl.pallas_call(
        functools.partial(second_kernel, n, cells),
        out_shape=(
            jax.ShapeDtypeStruct((n, depth, ranks, width), jnp.float32),
            jax.ShapeDtypeStruct((blocks * LANES, LANES), jnp.float32),
        ),
        in_specs=[VMEM, VMEM],
        out_specs=(VMEM, VMEM),
        scratch_shapes=[
            pltpu.VMEM((depth, n, ranks, width), jnp.float32),
            pltpu.VMEM((n, depth, ranks, width), jnp.float32),
            pltpu.SemaphoreType.DMA((count,)),
            pltpu.SemaphoreType.DMA((count,)),
        ],
        compiler_params=pltpu.CompilerParams(collective_id=1, has_side_effects=True),
    )(factor, fibres)


def local(nx, ny, nz, species_field, start_first, start_second):
    depth, rows, columns = species_field.shape
    rank, extent = start_first.shape[1], start_second.shape[0]
    species, ranks = S // nx, rank // ny
    cells = LANES // species
    fits = (
        columns % (nx * LANES) == 0
        and columns // nx == extent
        and species == ny
        and extent % LANES == 0
        and nx * rows % LANES == 0
        and ranks % 8 == 0
    )
    if not fits:
        return local_general(nx, ny, nz, species_field, start_first, start_second)
    axes, sizes = ("gz", "gy", "gx"), (nz, ny, nx)
    fibres, partial_first = first_stage(species_field, nx)
    gram_first = all_reduce(partial_first, axes, sizes, 2)
    factor_first = pl.pallas_call(
        first_power_kernel,
        out_shape=jax.ShapeDtypeStruct((rank, nx * rows), jnp.float32),
        in_specs=[VMEM, VMEM],
        out_specs=VMEM,
    )(gram_first, start_first.T)
    rows_second, partial_second = second_stage(factor_first, fibres, ny, cells)
    gram_second = all_reduce(partial_second, axes, sizes, 3)
    rows_second = rows_second.reshape(species * depth * ranks, extent)
    factor_second, core = pl.pallas_call(
        functools.partial(second_power_kernel, ny, cells),
        out_shape=(
            jax.ShapeDtypeStruct((rank, extent), jnp.float32),
            jax.ShapeDtypeStruct((rows_second.shape[0], rank), jnp.float32),
        ),
        in_specs=[VMEM, VMEM, VMEM],
        out_specs=(VMEM, VMEM),
    )(gram_second, start_second.T, rows_second)
    return (factor_first.T, factor_second.T, core.reshape(species, depth, ranks, rank))


def solution(mesh):
    return jax.shard_map(
        functools.partial(local, mesh.shape["gx"], mesh.shape["gy"], mesh.shape["gz"]),
        mesh=mesh,
        in_specs=(P("gz", "gx", "gy"), P(), P()),
        out_specs=(P(), P(), P("gx", "gz", "gy", None)),
        check_vma=False,
    )
```

```python
import functools

import jax
import jax.numpy as jnp
from jax import lax
from jax.experimental import pallas as pl
from jax.experimental.pallas import tpu as pltpu
from jax.sharding import PartitionSpec as P

S = 16
ITERS = 2
PANEL = 16
LANES = 128
MESH = pl.DeviceIdType.MESH
VMEM = pl.BlockSpec(memory_space=pltpu.VMEM)

exact_precision = lax.Precision.HIGHEST


def dot_dims(a, b, contract_a, contract_b):
    return lax.dot_general(
        a, b, (((contract_a,), (contract_b,)), ((), ())),
        precision=exact_precision, preferred_element_type=jnp.float32,
    )


def partners(n, me):
    if n == 4:
        return [3 - me, lax.rem(me + 2, 4), me + 1 - 2 * lax.rem(me, 2)]
    return [lax.rem(me + d, n) for d in range(1, n)]


def send(src, dst, send_sem, recv_sem, target):
    copy = pltpu.make_async_remote_copy(
        src_ref=src, dst_ref=dst, send_sem=send_sem, recv_sem=recv_sem,
        device_id=target, device_id_type=MESH,
    )
    copy.start()
    return copy


def say_hello(targets):
    barrier = pltpu.get_barrier_semaphore()
    for target in targets:
        pl.semaphore_signal(barrier, inc=1, device_id=target, device_id_type=MESH)


def hear_hello(targets):
    pl.semaphore_wait(pltpu.get_barrier_semaphore(), len(targets))


def greet(targets):
    say_hello(targets)
    hear_hello(targets)


def axis_peers(axes, sizes):
    return [{axis: p} for axis, n in zip(axes, sizes) for p in partners(n, lax.axis_index(axis))]


def reduce_blocks(axes, sizes, splits, x_ref, o_ref, scratch):
    levels = len(axes)
    landing, totals = scratch[:levels], scratch[levels : 2 * levels - 1]
    send_sems, recv_sems = scratch[2 * levels - 1 :]
    me = [lax.axis_index(axis) for axis in axes]
    peers = [partners(n, m) for n, m in zip(sizes, me)]
    spot = [m if split > 1 else 0 for m, split in zip(me, splits)]
    sem = 0
    held = x_ref
    for level in range(levels):
        axis, n, split = axes[level], sizes[level], splits[level]
        land = landing[level]
        copies = []
        for p in peers[level]:
            src = held.at[p] if split > 1 else held.at[0]
            copies.append(send(src, land.at[me[level]], send_sems.at[sem], recv_sems.at[sem], {axis: p}))
            sem += 1
        land[me[level]] = held[spot[level]]
        for copy in copies:
            copy.wait()
        total = land[0]
        for source in range(1, n):
            total = total + land[source]
        if level < levels - 1:
            totals[level][...] = total
            held = totals[level]
        else:
            o_ref[tuple(spot)] = total

    for level in reversed(range(levels)):
        if splits[level] == 1:
            continue
        block = o_ref.at[tuple(spot[: level + 1])]
        copies = []
        for p in peers[level]:
            copies.append(send(block, block, send_sems.at[sem], recv_sems.at[sem], {axes[level]: p}))
            sem += 1
        for copy in copies:
            copy.wait()


def all_reduce_kernel(axes, sizes, splits, x_ref, o_ref, *scratch):
    greet(axis_peers(axes, sizes))
    reduce_blocks(axes, sizes, splits, x_ref, o_ref, scratch)


def reduce_plan(rows, columns, sizes):
    splits = []
    for n in sizes:
        splits.append(n if rows % n == 0 else 1)
        rows //= splits[-1]
    scratch = [
        pltpu.VMEM((n, *splits[level + 1 :], rows, columns), jnp.float32)
        for level, n in enumerate(sizes)
    ]
    scratch += [pltpu.VMEM((*splits[level + 1 :], rows, columns), jnp.float32) for level in range(len(sizes) - 1)]
    count = sum(n - 1 for n in sizes) + sum(n - 1 for n, split in zip(sizes, splits) if split > 1)
    scratch += [pltpu.SemaphoreType.DMA((count,)), pltpu.SemaphoreType.DMA((count,))]
    return splits, (*splits, rows, columns), scratch


def all_reduce(x, axes, sizes, collective_id):
    splits, blocked, scratch = reduce_plan(*x.shape, sizes)
    out = pl.pallas_call(
        functools.partial(all_reduce_kernel, axes, sizes, splits),
        out_shape=jax.ShapeDtypeStruct(blocked, jnp.float32),
        in_specs=[VMEM],
        out_specs=VMEM,
        scratch_shapes=scratch,
        compiler_params=pltpu.CompilerParams(collective_id=collective_id, has_side_effects=True),
    )(x.reshape(blocked))
    return out.reshape(x.shape)


def fibres_kernel(n, x_ref, o_ref, send_sems, recv_sems):
    me = lax.axis_index("gx")
    depth, rows, width = x_ref.shape[0], x_ref.shape[1], o_ref.shape[-1]
    peers = partners(n, me)
    greet([{"gx": p} for p in peers])
    copies = []
    for turn, p in enumerate(peers):
        columns = pl.ds(pl.multiple_of(p * width, width), width)
        copies.append(
            send(x_ref.at[:, :, columns], o_ref.at[:, me], send_sems.at[turn], recv_sems.at[turn], {"gx": p})
        )
    own = pl.ds(pl.multiple_of(me * width, width), width)
    for level in range(depth):
        o_ref[level, me] = x_ref[level, :, own]
    for copy in copies:
        copy.wait()


def gather_fibres(field, n):
    depth, rows, columns = field.shape
    width = columns // n
    if width % 128:
        return lax.all_to_all(field, "gx", split_axis=2, concat_axis=1, tiled=True)
    out = pl.pallas_call(
        functools.partial(fibres_kernel, n),
        out_shape=jax.ShapeDtypeStruct((depth, n, rows, width), jnp.float32),
        in_specs=[VMEM],
        out_specs=VMEM,
        scratch_shapes=[pltpu.SemaphoreType.DMA((n - 1,)), pltpu.SemaphoreType.DMA((n - 1,))],
        compiler_params=pltpu.CompilerParams(collective_id=0, has_side_effects=True),
    )(field)
    return out.reshape(depth, n * rows, width)


def exchange_kernel(nx, ny, x_ref, o_ref, send_sems, recv_sems):
    mx, my = lax.axis_index("gx"), lax.axis_index("gy")
    peers = [(px, my) for px in partners(nx, mx)]
    for py in partners(ny, my):
        peers += [(px, py) for px in partners(nx, mx) + [mx]]
    greet([{"gx": px, "gy": py} for px, py in peers])
    copies = []
    for turn, (px, py) in enumerate(peers):
        copies.append(
            send(x_ref.at[py, px], o_ref.at[my, mx], send_sems.at[turn], recv_sems.at[turn], {"gx": px, "gy": py})
        )
    o_ref[my, mx] = x_ref[my, mx]
    for copy in copies:
        copy.wait()


def exchange(blocks):
    ny, nx = blocks.shape[:2]
    count = nx * ny - 1
    return pl.pallas_call(
        functools.partial(exchange_kernel, nx, ny),
        out_shape=jax.ShapeDtypeStruct(blocks.shape, jnp.float32),
        in_specs=[VMEM],
        out_specs=VMEM,
        scratch_shapes=[pltpu.SemaphoreType.DMA((count,)), pltpu.SemaphoreType.DMA((count,))],
        compiler_params=pltpu.CompilerParams(collective_id=1, has_side_effects=True),
    )(blocks)


def inverse_lower(cross):
    rank = cross.shape[0]
    panel = PANEL if rank % PANEL == 0 else 8
    row = lax.broadcasted_iota(jnp.int32, (rank, rank), 0)
    column = lax.broadcasted_iota(jnp.int32, (rank, rank), 1)
    rest = cross
    rest_inverse = jnp.where(row == column, 1.0, 0.0).astype(jnp.float32)
    local_row = lax.broadcasted_iota(jnp.int32, (panel, rank), 0)
    done = []
    for start in range(0, rank, panel):
        upper = rest[:panel]
        inverse = rest_inverse[:panel]
        columns = [
            jnp.broadcast_to(upper[:, start + j : start + j + 1], (panel, rank)) for j in range(panel)
        ]
        diagonal = jnp.ones((panel, rank), jnp.float32)
        for j in range(panel):
            pivot = jnp.broadcast_to(columns[j][j : j + 1], (panel, rank))
            diagonal = jnp.where(local_row == j, pivot, diagonal)
            if j == panel - 1:
                break
            factor = jnp.where(local_row > j, columns[j] * (1.0 / pivot), 0.0)
            for other in range(j + 1, panel):
                columns[other] = columns[other] - factor * columns[other][j : j + 1]
            upper = upper - factor * upper[j : j + 1]
            inverse = inverse - factor * inverse[j : j + 1]
        done.append(inverse * (1.0 / jnp.sqrt(diagonal)))
        if start + panel < rank:
            scaled = upper / diagonal
            update = dot_dims(scaled, jnp.concatenate([upper, inverse], axis=1), 0, 0)
            after = start + panel
            rest = rest[panel:] - update[after:, :rank]
            rest_inverse = rest_inverse[panel:] - update[after:, rank:]
    return jnp.concatenate(done, axis=0)


def power_general_kernel(gram_ref, start_ref, out_ref):
    current = start_ref[...]
    for turn in range(ITERS):
        images = dot_dims(gram_ref[...], current, 1, 0)
        cross = dot_dims(images, images, 0, 0)
        current = dot_dims(images, inverse_lower(cross), 1, 1)
    out_ref[...] = current


def leading(gram, start):
    return pl.pallas_call(
        power_general_kernel,
        out_shape=jax.ShapeDtypeStruct(start.shape, jnp.float32),
        in_specs=[VMEM, VMEM],
        out_specs=VMEM,
    )(gram, start)


def local_general(nx, ny, nz, species_field, start_first, start_second):
    axes, sizes = ("gz", "gy", "gx"), (nz, ny, nx)
    fibres = gather_fibres(species_field, nx)
    partial_gram = jnp.einsum("zic,zjc->ij", fibres, fibres, precision=exact_precision)
    gram_first = all_reduce(partial_gram, axes, sizes, 2)
    factor_first = leading(gram_first, start_first)

    depth = fibres.shape[0]
    cells = fibres.shape[2] // S
    rank = start_first.shape[1]
    species, ranks = S // nx, rank // ny
    projected = jnp.einsum("zim,ir->zmr", fibres, factor_first, precision=exact_precision)
    blocks = projected.reshape(depth, cells, nx, species, ny, ranks)
    blocks = blocks.transpose(4, 2, 1, 3, 0, 5).reshape(ny, nx, cells, species * depth * ranks)
    columns = exchange(blocks)
    columns = columns.reshape(ny * nx * cells, species * depth * ranks)
    partial_second = dot_dims(columns, columns, 1, 1)
    gram_second = all_reduce(partial_second, axes, sizes, 3)
    factor_second = leading(gram_second, start_second)
    core = dot_dims(columns, factor_second, 0, 0)
    core = core.reshape(species, depth, ranks, factor_second.shape[1])
    return (factor_first, factor_second, core)


def upper_blocks(count):
    return [(a, b) for a in range(count) for b in range(a, count)]


def add_gram(gram_ref, parts, contract, first):
    for slot, (a, b) in enumerate(upper_blocks(len(parts))):
        block = pl.ds(slot * LANES, LANES)
        term = dot_dims(parts[a], parts[b], contract, contract)
        gram_ref[block, :] = term if first else gram_ref[block, :] + term


def times_gram(current, gram_ref):
    count = current.shape[1] // LANES
    sums = [None] * count
    for slot, (a, b) in enumerate(upper_blocks(count)):
        block = gram_ref[slot * LANES : (slot + 1) * LANES, :]
        terms = [(b, a, 0)] if a == b else [(b, a, 0), (a, b, 1)]
        for to, of, contract in terms:
            term = dot_dims(current[:, of * LANES : (of + 1) * LANES], block, 1, contract)
            sums[to] = term if sums[to] is None else sums[to] + term
    return jnp.concatenate(sums, axis=1)


def power_steps(gram_ref, current):
    for turn in range(ITERS):
        images = times_gram(current, gram_ref)
        cross = dot_dims(images, images, 1, 1)
        current = dot_dims(inverse_lower(cross), images, 1, 0)
    return current


def second_power_kernel(groups, cells, gram_ref, start_ref, rows_ref, out_ref, core_ref):
    extent = start_ref.shape[1]
    chunks = extent // LANES
    true = lax.broadcasted_iota(jnp.int32, (extent, extent), 0)
    held = lax.broadcasted_iota(jnp.int32, (extent, extent), 1)
    shift = cells.bit_length() - 1
    chunk = lax.shift_right_logical(held, LANES.bit_length() - 1)
    group = lax.shift_right_logical(held & (LANES - 1), shift)
    order = jnp.where(true == (group * chunks + chunk) * cells + (held & (cells - 1)), 1.0, 0.0)
    current = power_steps(gram_ref, dot_dims(start_ref[...], order, 1, 0))
    out_ref[...] = dot_dims(current, order, 1, 1)
    core_ref[...] = dot_dims(rows_ref[...], current, 1, 1)


def species_major(block, order):
    high = block.astype(jnp.bfloat16)
    left = block - high.astype(jnp.float32)
    middle = left.astype(jnp.bfloat16)
    low = (left - middle.astype(jnp.float32)).astype(jnp.bfloat16)
    moved = [
        lax.dot_general(part, order, (((1,), (0,)), ((), ())), preferred_element_type=jnp.float32)
        for part in (high, middle, low)
    ]
    return (moved[0] + moved[1]) + moved[2]


def first_exchange(n, targets, x_ref, field, fibres, gram, packed, load_sems, send_sems, recv_sems):
    me = lax.axis_index("gx")
    depth, rows, columns = field.shape
    span = n * LANES
    cells = span // S
    width = columns // n
    loads = [pltpu.make_async_copy(x_ref.at[z], field.at[z], load_sems.at[z]) for z in range(depth)]
    for load in loads:
        load.start()
    say_hello(targets)
    peers = partners(n, me)
    source = lax.broadcasted_iota(jnp.int32, (span, span), 0)
    target = lax.broadcasted_iota(jnp.int32, (span, span), 1)
    species = lax.shift_right_logical(target, cells.bit_length() - 1)
    order = jnp.where(source == (target & (cells - 1)) * S + species, 1.0, 0.0).astype(jnp.bfloat16)
    copies = []
    for level in range(depth):
        loads[level].wait()
        for chunk in range(columns // span):
            moved = species_major(field[level, :, chunk * span : (chunk + 1) * span], order)
            lanes = pl.ds(chunk * LANES, LANES)
            for p in range(n):
                packed[level, p, :, lanes] = moved[:, p * LANES : (p + 1) * LANES]
        if level == 0:
            hear_hello(targets)
        turns = list(enumerate(peers))
        if level > 0:
            turns = turns[-1:] + turns[:-1]
        for turn, p in turns:
            sem = level * (n - 1) + turn
            copies.append(
                send(packed.at[level, p], fibres.at[level, me], send_sems.at[sem], recv_sems.at[sem], {"gx": p})
            )
        fibres[level, me] = packed[level, me]
    for level in range(depth):
        for copy in copies[level * (n - 1) : (level + 1) * (n - 1)]:
            copy.wait()
        whole = fibres[level].reshape(n * rows, width)
        parts = [whole[a : a + LANES] for a in range(0, n * rows, LANES)]
        add_gram(gram, parts, 1, level == 0)


def second_exchange(n, cells, factor, fibres, rows_ref, gram, packed, land, send_sems, recv_sems):
    me = lax.axis_index("gy")
    depth, ranks, width = packed.shape[0], packed.shape[2], packed.shape[3]
    peers = partners(n, me)
    copies = []
    for level in range(depth):
        whole = fibres[level].reshape(factor.shape[1], width)
        packed[level] = dot_dims(factor, whole, 1, 0).reshape(n, ranks, width)
        for turn, p in enumerate(peers):
            sem = level * (n - 1) + turn
            copies.append(
                send(packed.at[level, p], land.at[me, level], send_sems.at[sem], recv_sems.at[sem], {"gy": p})
            )
        land[me, level] = packed[level, me]
    lane_group = lax.shift_right_logical(
        lax.broadcasted_iota(jnp.int32, (ranks, LANES), 1), cells.bit_length() - 1
    )
    for level in range(depth):
        for copy in copies[level * (n - 1) : (level + 1) * (n - 1)]:
            copy.wait()
        for chunk in range(width // LANES):
            lanes = pl.ds(chunk * LANES, LANES)
            pieces = [land[t, level, :, lanes] for t in range(n)]
            for s in range(n):
                merged = pieces[s]
                for t in range(n):
                    if t != s:
                        turned = pltpu.roll(pieces[t], cells * ((t - s) % n), 1)
                        merged = jnp.where(lane_group == t, turned, merged)
                rows_ref[s, level, :, lanes] = merged
        whole = rows_ref[:, level].reshape(n * ranks, width)
        parts = [whole[:, a : a + LANES] for a in range(0, width, LANES)]
        add_gram(gram, parts, 0, level == 0)


def stages_kernel(axes, sizes, cells, splits, x_ref, start_ref, factor_ref, rows_ref, gram_ref, *scratch):
    ny, nx = sizes[1], sizes[2]
    targets = axis_peers(axes, sizes)
    gram, field, fibres, packed, load_sems, send_first, recv_first = scratch[:7]
    packed_second, land, send_second, recv_second = scratch[7:11]
    half = (len(scratch) - 11) // 2
    reduces = scratch[11 : 11 + half], scratch[11 + half :]

    def reduced(reduce_scratch, into):
        held, total = reduce_scratch[0], reduce_scratch[1]
        held[...] = gram[...].reshape(held.shape)
        reduce_blocks(axes, sizes, splits, held, total, reduce_scratch[2:])
        into[...] = total[...].reshape(into.shape)

    first_exchange(nx, targets, x_ref, field, fibres, gram, packed, load_sems, send_first, recv_first)
    reduced(reduces[0], gram)
    factor = power_steps(gram, start_ref[...])
    factor_ref[...] = factor
    second_exchange(ny, cells, factor, fibres, rows_ref, gram, packed_second, land, send_second, recv_second)
    reduced(reduces[1], gram_ref)


def stages(field, start, axes, sizes, cells):
    ny, nx = sizes[1], sizes[2]
    depth, rows, columns = field.shape
    rank, extent = start.shape
    width = columns // nx
    ranks = rank // ny
    gram_shape = (len(upper_blocks(extent // LANES)) * LANES, LANES)
    splits, blocked, reduce_scratch = reduce_plan(*gram_shape, sizes)
    reduce_scratch = [pltpu.VMEM(blocked, jnp.float32)] * 2 + reduce_scratch
    first, second = depth * (nx - 1), depth * (ny - 1)
    return pl.pallas_call(
        functools.partial(stages_kernel, axes, sizes, cells, splits),
        out_shape=(
            jax.ShapeDtypeStruct((rank, extent), jnp.float32),
            jax.ShapeDtypeStruct((ny, depth, ranks, width), jnp.float32),
            jax.ShapeDtypeStruct(gram_shape, jnp.float32),
        ),
        in_specs=[pl.BlockSpec(memory_space=pl.ANY), VMEM],
        out_specs=(VMEM, VMEM, VMEM),
        scratch_shapes=[
            pltpu.VMEM(gram_shape, jnp.float32),
            pltpu.VMEM((depth, rows, columns), jnp.float32),
            pltpu.VMEM((depth, nx, rows, width), jnp.float32),
            pltpu.VMEM((depth, nx, rows, width), jnp.float32),
            pltpu.SemaphoreType.DMA((depth,)),
            pltpu.SemaphoreType.DMA((first,)),
            pltpu.SemaphoreType.DMA((first,)),
            pltpu.VMEM((depth, ny, ranks, width), jnp.float32),
            pltpu.VMEM((ny, depth, ranks, width), jnp.float32),
            pltpu.SemaphoreType.DMA((second,)),
            pltpu.SemaphoreType.DMA((second,)),
            *reduce_scratch,
            *reduce_scratch,
        ],
        compiler_params=pltpu.CompilerParams(collective_id=0, has_side_effects=True),
    )(field, start)


def local(nx, ny, nz, species_field, start_first, start_second):
    depth, rows, columns = species_field.shape
    rank, extent = start_first.shape[1], start_second.shape[0]
    species, ranks = S // nx, rank // ny
    cells = LANES // species
    fits = (
        columns % (nx * LANES) == 0
        and columns // nx == extent
        and nx * rows == extent
        and species == ny
        and extent % LANES == 0
        and nx * rows % LANES == 0
        and ranks % 8 == 0
    )
    if not fits:
        return local_general(nx, ny, nz, species_field, start_first, start_second)
    axes, sizes = ("gz", "gy", "gx"), (nz, ny, nx)
    factor_first, rows_second, gram_second = stages(species_field, start_first.T, axes, sizes, cells)
    rows_second = rows_second.reshape(species * depth * ranks, extent)
    factor_second, core = pl.pallas_call(
        functools.partial(second_power_kernel, ny, cells),
        out_shape=(
            jax.ShapeDtypeStruct((rank, extent), jnp.float32),
            jax.ShapeDtypeStruct((rows_second.shape[0], rank), jnp.float32),
        ),
        in_specs=[VMEM, VMEM, VMEM],
        out_specs=(VMEM, VMEM),
    )(gram_second, start_second.T, rows_second)
    return (factor_first.T, factor_second.T, core.reshape(species, depth, ranks, rank))


def solution(mesh):
    return jax.shard_map(
        functools.partial(local, mesh.shape["gx"], mesh.shape["gy"], mesh.shape["gz"]),
        mesh=mesh,
        in_specs=(P("gz", "gx", "gy"), P(), P()),
        out_specs=(P(), P(), P("gx", "gz", "gy", None)),
        check_vma=False,
    )
```
